32 devices in a mesh: clip: 16 (over z, y, core), frame: 2 (over x).
Axes of the slice: x: 2, y: 2, z: 4, core: 2. Of those that a mesh axis runs over, the one named last changes fastest.
Arguments:
- layer_input: bfloat16 [16, 376, 768], P('clip', 'frame'), may hold values from -6 to 6
- w_qkv: bfloat16 [768, 2304], P(('clip', 'frame')), may hold values from -0.21875 to 0.21875
- b_q: bfloat16 [768], P(('clip', 'frame')), may hold values from -1.75 to 1.75
- b_v: bfloat16 [768], P(('clip', 'frame')), may hold values from -0.125 to 0.125
- w_out: bfloat16 [768, 768], P(('clip', 'frame')), may hold values from -6 to 6
- b_out: bfloat16 [768], P(('clip', 'frame')), may hold values from -1.75 to 1.75
- ln1_gain: bfloat16 [768], P(('clip', 'frame')), may hold values from 0.25 to 1.75
- ln1_bias: bfloat16 [768], P(('clip', 'frame')), may hold values from -1.25 to 1.25
- ln2_gain: bfloat16 [768], P(('clip', 'frame')), may hold values from 0.25 to 1.75
- ln2_bias: bfloat16 [768], P(('clip', 'frame')), may hold values from -1.25 to 1.25
- w_up: bfloat16 [768, 3072], P(('clip', 'frame')), may hold values from -0.21875 to 0.21875
- b_up: bfloat16 [3072], P(('clip', 'frame')), may hold values from -1.75 to 1.75
- w_down: bfloat16 [3072, 768], P(('clip', 'frame')), may hold values from -0.109375 to 0.109375
- b_down: bfloat16 [768], P(('clip', 'frame')), may hold values from -1.75 to 1.75
- grad_y: bfloat16 [16, 376, 768], P('clip', 'frame'), may hold values from -6 to 6
- pad_mask: int32 [16, 376], replicated, may hold values from 0 to 1, as said below
- clip_row: int32 [16], replicated, may hold values from 0 to 15, each once
Outputs:
- layer_out: bfloat16 [16, 376, 768], P('clip', 'frame')
- d_x: float32 [16, 376, 768], P('clip', 'frame')
- d_w_qkv: float32 [768, 2304], P(('clip', 'frame'))
- d_b_q: float32 [768], P(('clip', 'frame'))
- d_b_v: float32 [768], P(('clip', 'frame'))
- d_w_out: float32 [768, 768], P(('clip', 'frame'))
- d_b_out: float32 [768], P(('clip', 'frame'))
- d_ln1_gain: float32 [768], P(('clip', 'frame'))
- d_ln1_bias: float32 [768], P(('clip', 'frame'))
- d_ln2_gain: float32 [768], P(('clip', 'frame'))
- d_ln2_bias: float32 [768], P(('clip', 'frame'))
- d_w_up: float32 [768, 3072], P(('clip', 'frame'))
- d_b_up: float32 [3072], P(('clip', 'frame'))
- d_w_down: float32 [3072, 768], P(('clip', 'frame'))
- d_b_down: float32 [768], P(('clip', 'frame'))
The draws below stay inside these ranges and needn't reach their ends.
Inputs may be any that keep to these rules, and one draw needn't show every extreme that they name: `pad_mask`: each clip's mask is 1 on a leading run of L frames and 0 after it, with 188 <= L <= 372; some clip has each of the two extreme lengths. `clip_row`: each clip stands in exactly one row.
All inputs are finite; a program needn't handle non-finite values.
Results may differ from the reference program's by a relative error of at most 0.01.
Values may be sent and summed in bfloat16 or wider, within the bound.
No kernel may reach another device: no remote copies, remote signals or barrier semaphores. Data moves between devices by JAX's collectives and lax.ppermute only.
A program may use at most 192 MiB of HBM per device.

```python
import math
import jax
import jax.numpy as jnp
from jax import lax

D = 768
HEADS = 12
HEAD_DIM = 64
FF = 3072
CLIPS = 16
FRAMES = 376


def draw_pad_mask(key, part):
    first, second = jax.random.split(jax.random.fold_in(key, 23), 2)
    lowest = FRAMES // 2
    highest = FRAMES - 4
    lengths = jax.random.randint(first, (CLIPS,), lowest, highest + 1)
    order = jax.random.permutation(second, CLIPS)
    lengths = lengths.at[order[0]].set(highest)
    lengths = lengths.at[order[1]].set(lowest)
    positions = jnp.arange(FRAMES, dtype=jnp.int32)
    return (positions[None, :] < lengths[:, None]).astype(jnp.int32)


def level_of(key, extent, pieces, smallest, largest):
    def one(position, shards_of):
        draws = jax.random.uniform(jax.random.fold_in(jax.random.fold_in(key, 6), position), (shards_of,), jnp.float32, smallest / len(pieces), largest / len(pieces))
        return jnp.repeat(jnp.exp(draws), extent[position] // shards_of).reshape((-1,) + (1,) * (len(extent) - position - 1))

    factor_of = one(*pieces[0])
    for cut in pieces[1:]:
        factor_of = factor_of * one(*cut)
    return factor_of


def normal_values(stream_key, extent, spread, most, shards=(), kind=jnp.bfloat16):
    factor_of = level_of(stream_key, extent, shards, -0.22, 0.18) if shards else 1.0
    drawn = jax.random.normal(stream_key, extent, jnp.float32) * spread * factor_of
    return jnp.minimum(jnp.maximum(drawn, -most), most).astype(kind)


def setup_inputs(seed: int = 0) -> dict:
    splits = jax.random.split(jax.random.key(seed), 18)
    layer_input = normal_values(splits[0], (CLIPS, FRAMES, D), 1.0, 6.0, ((0, 16), (1, 2)))
    w_qkv = normal_values(splits[1], (D, 3 * D), D ** -0.5, 0.21875, ((0, 32),))
    b_q = normal_values(splits[2], (D,), 0.3, 1.75, ((0, 32),))
    b_v = normal_values(splits[3], (D,), 0.02, 0.125, ((0, 32),))
    w_out = normal_values(splits[4], (D, D), (FRAMES ** 0.5 * D ** -0.5), 6.0, ((0, 32),))
    b_out = normal_values(splits[5], (D,), 0.3, 1.75, ((0, 32),))
    ln1_gain = jnp.clip(1.0 + 0.15 * jax.random.normal(splits[6], (D,), jnp.float32), 0.25, 1.75).astype(jnp.bfloat16)
    ln1_bias = normal_values(splits[7], (D,), 0.2, 1.25, ((0, 32),))
    ln2_gain = jnp.clip(1.0 + 0.15 * jax.random.normal(splits[8], (D,), jnp.float32), 0.25, 1.75).astype(jnp.bfloat16)
    ln2_bias = normal_values(splits[9], (D,), 0.2, 1.25, ((0, 32),))
    w_up = normal_values(splits[10], (D, FF), D ** -0.5, 0.21875, ((0, 32),))
    b_up = normal_values(splits[11], (FF,), 0.3, 1.75, ((0, 32),))
    w_down = normal_values(splits[12], (FF, D), FF ** -0.5, 0.109375, ((0, 32),))
    b_down = normal_values(splits[13], (D,), 0.3, 1.75, ((0, 32),))
    grad_y = normal_values(splits[14], (CLIPS, FRAMES, D), 1.0, 6.0, ((0, 16), (1, 2)))
    pad_mask = draw_pad_mask(jax.random.fold_in(splits[17], 71), 0)
    clip_row = jax.random.permutation(splits[16], CLIPS).astype(jnp.int32)
    return {"layer_input": layer_input, "w_qkv": w_qkv, "b_q": b_q, "b_v": b_v, "w_out": w_out, "b_out": b_out, "ln1_gain": ln1_gain, "ln1_bias": ln1_bias, "ln2_gain": ln2_gain, "ln2_bias": ln2_bias, "w_up": w_up, "b_up": b_up, "w_down": w_down, "b_down": b_down, "grad_y": grad_y, "pad_mask": pad_mask, "clip_row": clip_row}


EPS = 1e-05

def normalize(values):
    centered = values - lax.optimization_barrier(jnp.mean(values, axis=-1, keepdims=True))
    factor = lax.rsqrt(lax.optimization_barrier(jnp.mean(centered * centered, axis=-1, keepdims=True)) + EPS)
    return (centered * factor, factor)

def norm_back(grad_hat, normed, factor):
    return factor * (grad_hat - lax.optimization_barrier(jnp.mean(grad_hat, axis=-1, keepdims=True)) - normed * lax.optimization_barrier(jnp.mean(grad_hat * normed, axis=-1, keepdims=True)))

def gelu_exact(values):
    return 0.5 * values * (1.0 + jax.scipy.special.erf(values * 0.7071067811865476))

def gelu_slope(values):
    return 0.5 * (1.0 + jax.scipy.special.erf(values * 0.7071067811865476)) + values * jnp.exp(-0.5 * values * values) * 0.3989422804014327

def rounded(values):
    return lax.optimization_barrier(values.astype(jnp.bfloat16)).astype(jnp.float32)

def matmul(left, right):
    return jnp.dot(left, right, preferred_element_type=jnp.float32)

def reference(layer_input, w_qkv, b_q, b_v, w_out, b_out, ln1_gain, ln1_bias, ln2_gain, ln2_bias, w_up, b_up, w_down, b_down, grad_y, pad_mask, clip_row):
    scale = 1.0 / math.sqrt(HEAD_DIM)
    mask_rows = jnp.take(pad_mask, clip_row.astype(jnp.int32), axis=0)
    query_bias = b_q.astype(jnp.float32)
    value_bias = b_v.astype(jnp.float32)
    out_bias = b_out.astype(jnp.float32)
    gain_one = ln1_gain.astype(jnp.float32)
    shift_one = ln1_bias.astype(jnp.float32)
    gain_two = ln2_gain.astype(jnp.float32)
    shift_two = ln2_bias.astype(jnp.float32)
    up_bias = b_up.astype(jnp.float32)
    down_bias = b_down.astype(jnp.float32)

    def one_clip(totals, inputs):
        clip_input, clip_grad, live = inputs
        inputs_f = clip_input.astype(jnp.float32)
        normed1, factor1 = normalize(inputs_f)
        hidden1 = (normed1 * gain_one + shift_one).astype(jnp.bfloat16)
        projected = matmul(hidden1, w_qkv)
        queries = rounded(projected[:, :D] + query_bias)
        keys_all = rounded(projected[:, D:2 * D])
        values_all = rounded(projected[:, 2 * D:] + value_bias)
        query_heads = queries.reshape(FRAMES, HEADS, HEAD_DIM)
        key_heads = keys_all.reshape(FRAMES, HEADS, HEAD_DIM)
        value_heads = values_all.reshape(FRAMES, HEADS, HEAD_DIM)
        scores = jnp.einsum('qhd,khd->hqk', query_heads, key_heads) * scale
        scores = jnp.where(live[None, None, :] > 0, scores, -1e+30)
        top = lax.optimization_barrier(jnp.max(scores, axis=-1, keepdims=True))
        lse = top + jnp.log(lax.optimization_barrier(jnp.sum(jnp.exp(scores - top), axis=-1, keepdims=True)))
        probs = jnp.exp(scores - lse)
        probs_b = rounded(probs)
        attended = jnp.einsum('hqk,khd->qhd', probs_b, value_heads).reshape(FRAMES, D)
        attended_b = attended.astype(jnp.bfloat16)
        resid = inputs_f + matmul(attended_b, w_out) + out_bias
        normed2, factor2 = normalize(resid)
        hidden2 = (normed2 * gain_two + shift_two).astype(jnp.bfloat16)
        pre = matmul(hidden2, w_up) + up_bias
        act = gelu_exact(pre).astype(jnp.bfloat16)
        output = (resid + matmul(act, w_down) + down_bias).astype(jnp.bfloat16)
        upstream = clip_grad.astype(jnp.float32)
        grad_down_bias = lax.optimization_barrier(jnp.sum(upstream, axis=0))
        grad_down = matmul(act.T, clip_grad)
        grad_pre = matmul(clip_grad, w_down.T) * gelu_slope(pre)
        grad_pre_b = grad_pre.astype(jnp.bfloat16)
        grad_up_bias = lax.optimization_barrier(jnp.sum(grad_pre, axis=0))
        grad_up = matmul(hidden2.T, grad_pre_b)
        grad_hidden2 = matmul(grad_pre_b, w_up.T)
        grad_gain_two = lax.optimization_barrier(jnp.sum(grad_hidden2 * normed2, axis=0))
        grad_shift_two = lax.optimization_barrier(jnp.sum(grad_hidden2, axis=0))
        grad_resid = upstream + norm_back(grad_hidden2 * gain_two, normed2, factor2)
        grad_resid_b = grad_resid.astype(jnp.bfloat16)
        grad_out_bias = lax.optimization_barrier(jnp.sum(grad_resid, axis=0))
        grad_out = matmul(attended_b.T, grad_resid_b)
        grad_att = rounded(matmul(grad_resid_b, w_out.T))
        grad_heads = grad_att.reshape(FRAMES, HEADS, HEAD_DIM)
        grad_probs = jnp.einsum('qhd,khd->hqk', grad_heads, value_heads)
        inner = lax.optimization_barrier(jnp.sum(probs * grad_probs, axis=-1, keepdims=True))
        grad_scores = rounded(probs * (grad_probs - inner) * scale)
        grad_queries = jnp.einsum('hqk,khd->qhd', grad_scores, key_heads).reshape(FRAMES, D)
        grad_keys = jnp.einsum('hqk,qhd->khd', grad_scores, query_heads).reshape(FRAMES, D)
        grad_values = jnp.einsum('hqk,qhd->khd', probs_b, grad_heads).reshape(FRAMES, D)
        grad_query_bias = lax.optimization_barrier(jnp.sum(grad_queries, axis=0))
        grad_value_bias = lax.optimization_barrier(jnp.sum(grad_values, axis=0))
        grad_proj = jnp.concatenate([grad_queries, grad_keys, grad_values], axis=-1).astype(jnp.bfloat16)
        grad_qkv = matmul(hidden1.T, grad_proj)
        grad_hidden1 = matmul(grad_proj, w_qkv.T)
        grad_gain_one = lax.optimization_barrier(jnp.sum(grad_hidden1 * normed1, axis=0))
        grad_shift_one = lax.optimization_barrier(jnp.sum(grad_hidden1, axis=0))
        grad_input = grad_resid + norm_back(grad_hidden1 * gain_one, normed1, factor1)
        terms = (grad_qkv, grad_query_bias, grad_value_bias, grad_out, grad_out_bias, grad_gain_one, grad_shift_one, grad_gain_two, grad_shift_two, grad_up, grad_up_bias, grad_down, grad_down_bias)
        summed = tuple((total + term for total, term in zip(totals, terms)))
        return (summed, (output, grad_input))
    empty = (jnp.zeros((D, 3 * D), jnp.float32), jnp.zeros((D,), jnp.float32), jnp.zeros((D,), jnp.float32), jnp.zeros((D, D), jnp.float32), jnp.zeros((D,), jnp.float32), jnp.zeros((D,), jnp.float32), jnp.zeros((D,), jnp.float32), jnp.zeros((D,), jnp.float32), jnp.zeros((D,), jnp.float32), jnp.zeros((D, FF), jnp.float32), jnp.zeros((FF,), jnp.float32), jnp.zeros((FF, D), jnp.float32), jnp.zeros((D,), jnp.float32))
    totals, stacked = lax.scan(one_clip, empty, (layer_input, grad_y, mask_rows))
    return (stacked[0], stacked[1], totals[0], totals[1], totals[2], totals[3], totals[4], totals[5], totals[6], totals[7], totals[8], totals[9], totals[10], totals[11], totals[12])
```

```python
import math

import jax
import jax.numpy as jnp
from jax import lax
from jax.experimental import pallas as pl
from jax.experimental.pallas import tpu as pltpu
from jax.sharding import PartitionSpec as P

HEADS = 12
HEAD_DIM = 64


EPS = 1e-05


def normalize(values):
    centered = values - jnp.mean(values, axis=-1, keepdims=True)
    factor = lax.rsqrt(jnp.mean(centered * centered, axis=-1, keepdims=True) + EPS)
    return (centered * factor, factor)


def norm_back(grad_hat, normed, factor):
    return factor * (
        grad_hat
        - jnp.mean(grad_hat, axis=-1, keepdims=True)
        - normed * jnp.mean(grad_hat * normed, axis=-1, keepdims=True)
    )


def gelu_exact(values):
    return 0.5 * values * (1.0 + jax.scipy.special.erf(values * 0.7071067811865476))


def gelu_slope(values):
    return (
        0.5 * (1.0 + jax.scipy.special.erf(values * 0.7071067811865476))
        + values * jnp.exp(-0.5 * values * values) * 0.3989422804014327
    )


def matmul(left, right):
    return jnp.dot(left, right, preferred_element_type=jnp.float32)


def general_body(
    layer_input,
    w_qkv,
    b_q,
    b_v,
    w_out,
    b_out,
    ln1_gain,
    ln1_bias,
    ln2_gain,
    ln2_bias,
    w_up,
    b_up,
    w_down,
    b_down,
    grad_y,
    pad_mask,
    clip_row,
):
    clips_here, frames_here, width = layer_input.shape
    tokens_here = clips_here * frames_here
    frames_all = frames_here * lax.axis_size("frame")
    scale = 1.0 / math.sqrt(HEAD_DIM)
    first_row = lax.axis_index("clip") * clips_here
    held = lax.dynamic_slice_in_dim(clip_row, first_row, clips_here)
    key_live = jnp.take(pad_mask, held, axis=0) > 0
    params = (
        lax.all_gather(w_qkv, ("clip", "frame"), axis=0, tiled=True),
        lax.all_gather(b_q, ("clip", "frame"), axis=0, tiled=True),
        lax.all_gather(b_v, ("clip", "frame"), axis=0, tiled=True),
        lax.all_gather(w_out, ("clip", "frame"), axis=0, tiled=True),
        lax.all_gather(b_out, ("clip", "frame"), axis=0, tiled=True),
        lax.all_gather(ln1_gain, ("clip", "frame"), axis=0, tiled=True),
        lax.all_gather(ln1_bias, ("clip", "frame"), axis=0, tiled=True),
        lax.all_gather(ln2_gain, ("clip", "frame"), axis=0, tiled=True),
        lax.all_gather(ln2_bias, ("clip", "frame"), axis=0, tiled=True),
        lax.all_gather(w_up, ("clip", "frame"), axis=0, tiled=True),
        lax.all_gather(b_up, ("clip", "frame"), axis=0, tiled=True),
        lax.all_gather(w_down, ("clip", "frame"), axis=0, tiled=True),
        lax.all_gather(b_down, ("clip", "frame"), axis=0, tiled=True),
    )
    (
        qkv_mat,
        query_bias,
        value_bias,
        out_mat,
        out_bias,
        gain_one,
        shift_one,
        gain_two,
        shift_two,
        up_mat,
        up_bias,
        down_mat,
        down_bias,
    ) = params
    inputs_f = layer_input.reshape(tokens_here, width).astype(jnp.float32)
    normed1, factor1 = normalize(inputs_f)
    hidden1 = (normed1 * gain_one.astype(jnp.float32) + shift_one.astype(jnp.float32)).astype(
        jnp.bfloat16
    )
    projected = matmul(hidden1, qkv_mat)
    queries = (projected[:, :width] + query_bias.astype(jnp.float32)).astype(jnp.bfloat16)
    keys_local = projected[:, width : 2 * width].astype(jnp.bfloat16)
    values_local = (projected[:, 2 * width :] + value_bias.astype(jnp.float32)).astype(jnp.bfloat16)
    pair_local = jnp.concatenate([keys_local, values_local], axis=-1).reshape(
        clips_here, frames_here, 2 * width
    )
    pair_all = lax.all_gather(pair_local, "frame", axis=1, tiled=True)
    query_heads = queries.reshape(clips_here, frames_here, HEADS, HEAD_DIM)

    def score_block(pair_full):
        key_heads = pair_full[..., :width].reshape(clips_here, frames_all, HEADS, HEAD_DIM)
        raw = (
            jnp.einsum(
                "cqhd,ckhd->chqk", query_heads, key_heads, preferred_element_type=jnp.float32
            )
            * scale
        )
        return jnp.where(key_live[:, None, None, :], raw, -1e30)

    scores = score_block(pair_all)
    top = jnp.max(scores, axis=-1, keepdims=True)
    lse = top + jnp.log(jnp.sum(jnp.exp(scores - top), axis=-1, keepdims=True))
    probs_b = jnp.exp(scores - lse).astype(jnp.bfloat16)
    value_heads = pair_all[..., width:].reshape(clips_here, frames_all, HEADS, HEAD_DIM)
    attended = jnp.einsum(
        "chqk,ckhd->cqhd", probs_b, value_heads, preferred_element_type=jnp.float32
    ).reshape(tokens_here, width)
    attended_b = attended.astype(jnp.bfloat16)
    resid = inputs_f + matmul(attended_b, out_mat) + out_bias.astype(jnp.float32)
    normed2, factor2 = normalize(resid)
    hidden2 = (normed2 * gain_two.astype(jnp.float32) + shift_two.astype(jnp.float32)).astype(
        jnp.bfloat16
    )
    pre = matmul(hidden2, up_mat) + up_bias.astype(jnp.float32)
    act = gelu_exact(pre).astype(jnp.bfloat16)
    output = (resid + matmul(act, down_mat) + down_bias.astype(jnp.float32)).astype(jnp.bfloat16)
    qkv_back = params[0]
    out_back = params[3]
    gain_one_back = params[5].astype(jnp.float32)
    gain_two_back = params[7].astype(jnp.float32)
    up_back = params[9]
    down_back = params[11]
    upstream = grad_y.reshape(tokens_here, width)
    upstream_f = upstream.astype(jnp.float32)
    grad_down_bias = jnp.sum(upstream_f, axis=0)
    grad_down = matmul(act.T, upstream)
    grad_pre = matmul(upstream, down_back.T) * gelu_slope(pre)
    grad_pre_b = grad_pre.astype(jnp.bfloat16)
    grad_up_bias = jnp.sum(grad_pre, axis=0)
    grad_up = matmul(hidden2.T, grad_pre_b)
    grad_hidden2 = matmul(grad_pre_b, up_back.T)
    grad_gain_two = jnp.sum(grad_hidden2 * normed2, axis=0)
    grad_shift_two = jnp.sum(grad_hidden2, axis=0)
    grad_resid = upstream_f + norm_back(grad_hidden2 * gain_two_back, normed2, factor2)
    grad_resid_b = grad_resid.astype(jnp.bfloat16)
    grad_out_bias = jnp.sum(grad_resid, axis=0)
    grad_out = matmul(attended_b.T, grad_resid_b)
    grad_att = matmul(grad_resid_b, out_back.T).astype(jnp.bfloat16)
    grad_heads = grad_att.reshape(clips_here, frames_here, HEADS, HEAD_DIM)
    scores_back = score_block(pair_all)
    probs = jnp.exp(scores_back - lse)
    probs_back_b = probs.astype(jnp.bfloat16)
    key_back = pair_all[..., :width].reshape(clips_here, frames_all, HEADS, HEAD_DIM)
    value_back = pair_all[..., width:].reshape(clips_here, frames_all, HEADS, HEAD_DIM)
    grad_probs = jnp.einsum(
        "cqhd,ckhd->chqk", grad_heads, value_back, preferred_element_type=jnp.float32
    )
    inner = jnp.sum(probs * grad_probs, axis=-1, keepdims=True)
    grad_scores = (probs * (grad_probs - inner) * scale).astype(jnp.bfloat16)
    grad_queries = jnp.einsum(
        "chqk,ckhd->cqhd", grad_scores, key_back, preferred_element_type=jnp.float32
    ).reshape(tokens_here, width)
    grad_keys_part = jnp.einsum(
        "chqk,cqhd->ckhd", grad_scores, query_heads, preferred_element_type=jnp.float32
    ).reshape(clips_here, frames_all, width)
    grad_values_part = jnp.einsum(
        "chqk,cqhd->ckhd", probs_back_b, grad_heads, preferred_element_type=jnp.float32
    ).reshape(clips_here, frames_all, width)
    grad_pair = lax.psum_scatter(
        jnp.concatenate([grad_keys_part, grad_values_part], axis=-1),
        "frame",
        scatter_dimension=1,
        tiled=True,
    )
    grad_pair = grad_pair.reshape(tokens_here, 2 * width)
    grad_query_bias = jnp.sum(grad_queries, axis=0)
    grad_value_bias = jnp.sum(grad_pair[:, width:], axis=0)
    grad_proj = jnp.concatenate([grad_queries, grad_pair], axis=-1).astype(jnp.bfloat16)
    grad_qkv = matmul(hidden1.T, grad_proj)
    grad_hidden1 = matmul(grad_proj, qkv_back.T)
    grad_gain_one = jnp.sum(grad_hidden1 * normed1, axis=0)
    grad_shift_one = jnp.sum(grad_hidden1, axis=0)
    grad_input = grad_resid + norm_back(grad_hidden1 * gain_one_back, normed1, factor1)
    shares = (
        lax.psum_scatter(grad_qkv, ("clip", "frame"), scatter_dimension=0, tiled=True),
        lax.psum_scatter(grad_query_bias, ("clip", "frame"), scatter_dimension=0, tiled=True),
        lax.psum_scatter(grad_value_bias, ("clip", "frame"), scatter_dimension=0, tiled=True),
        lax.psum_scatter(grad_out, ("clip", "frame"), scatter_dimension=0, tiled=True),
        lax.psum_scatter(grad_out_bias, ("clip", "frame"), scatter_dimension=0, tiled=True),
        lax.psum_scatter(grad_gain_one, ("clip", "frame"), scatter_dimension=0, tiled=True),
        lax.psum_scatter(grad_shift_one, ("clip", "frame"), scatter_dimension=0, tiled=True),
        lax.psum_scatter(grad_gain_two, ("clip", "frame"), scatter_dimension=0, tiled=True),
        lax.psum_scatter(grad_shift_two, ("clip", "frame"), scatter_dimension=0, tiled=True),
        lax.psum_scatter(grad_up, ("clip", "frame"), scatter_dimension=0, tiled=True),
        lax.psum_scatter(grad_up_bias, ("clip", "frame"), scatter_dimension=0, tiled=True),
        lax.psum_scatter(grad_down, ("clip", "frame"), scatter_dimension=0, tiled=True),
        lax.psum_scatter(grad_down_bias, ("clip", "frame"), scatter_dimension=0, tiled=True),
    )
    return (
        output.reshape(clips_here, frames_here, width),
        grad_input.reshape(clips_here, frames_here, width),
        shares[0],
        shares[1],
        shares[2],
        shares[3],
        shares[4],
        shares[5],
        shares[6],
        shares[7],
        shares[8],
        shares[9],
        shares[10],
        shares[11],
        shares[12],
    )


AXES = ("clip", "frame")
ANY = pl.BlockSpec(memory_space=pl.ANY)


def hop(value, dz=0, dy=0, dc=0, dx=0):
    flip = dz * 8 + dy * 4 + dc * 2 + dx
    return lax.ppermute(value, AXES, [(i, i ^ flip) for i in range(32)])


def my_shard():
    return lax.axis_index("clip") * 2 + lax.axis_index("frame")


def gather_pieces(shard):
    own = shard[None]
    near = hop(own, dz=1)
    far = hop(own, dz=2)
    across = hop(own, dz=3)
    first = jnp.concatenate([own, near], axis=0)
    second = jnp.concatenate([far, across], axis=0)
    first = jnp.concatenate([first, hop(first, dy=1)], axis=0)
    second = jnp.concatenate([second, hop(second, dx=1)], axis=0)
    first_x = hop(first, dx=1)
    second_y = hop(second, dy=1)
    arrays = (first, first_x, second, second_y)
    arrays = arrays + tuple(hop(array, dc=1) for array in arrays)
    flips = []
    for dc in (0, 1):
        for dx in (0, 1):
            flips.append([dz * 8 + dy * 4 + dc * 2 + dx for dy in (0, 1) for dz in (0, 1)])
        for dy in (0, 1):
            flips.append([dz * 8 + dy * 4 + dc * 2 + dx for dx in (0, 1) for dz in (2, 3)])
    return arrays, flips


def assemble(shard, name):
    arrays, flips = gather_pieces(shard)
    rows, cols = shard.shape

    def kernel(*refs):
        parts, out, sems = refs[:8], refs[8], refs[9]
        me = my_shard()
        copies = []
        for part, flip in zip(parts, flips):
            for k in range(4):
                copies.append(
                    pltpu.make_async_copy(
                        part.at[k], out.at[me ^ flip[k]], sems.at[len(copies)]
                    )
                )
        for copy in copies:
            copy.start()
        for copy in copies:
            copy.wait()

    whole = pl.pallas_call(
        kernel,
        name=name,
        out_shape=jax.ShapeDtypeStruct((32, rows, cols), shard.dtype),
        in_specs=[ANY] * 8,
        out_specs=pl.BlockSpec(memory_space=pltpu.VMEM),
        scratch_shapes=[pltpu.SemaphoreType.DMA((32,))],
    )(*arrays)
    return whole.reshape(32 * rows, cols)


def weight_grad(left, right, block, name):
    tokens, depth = left.shape
    cols = right.shape[1]
    rows = depth // 32
    slots = []
    for dc in (0, 1):
        slots.append([dz * 8 + dy * 4 + dc * 2 + dx for dx in (0, 1) for dy in (0, 1) for dz in (0, 1)])
        slots.append([dz * 8 + dy * 4 + dc * 2 + dx for dy in (0, 1) for dx in (0, 1) for dz in (2, 3)])

    def kernel(left_ref, right_ref, *refs):
        outs, total = refs[:4], refs[4]
        me = my_shard()
        total[...] = lax.dot_general(
            left_ref[...], right_ref[...], (((0,), (0,)), ((), ())), preferred_element_type=jnp.float32
        )
        for out, slot in zip(outs, slots):
            for k in range(8):
                start = pl.multiple_of((me ^ slot[k]) * rows, 8)
                out[k] = total[pl.ds(start, rows), :].astype(jnp.bfloat16)

    return pl.pallas_call(
        kernel,
        name=name,
        grid=(cols // block,),
        out_shape=[jax.ShapeDtypeStruct((8, rows, cols), jnp.bfloat16)] * 4,
        in_specs=[
            pl.BlockSpec((tokens, depth), lambda j: (0, 0)),
            pl.BlockSpec((tokens, block), lambda j: (0, j)),
        ],
        out_specs=[pl.BlockSpec((8, rows, block), lambda j: (0, 0, j))] * 4,
        scratch_shapes=[pltpu.VMEM((depth, block), jnp.float32)],
    )(left, right)


def wide(value):
    return value.astype(jnp.float32)


def narrow(value):
    return value.astype(jnp.bfloat16)


def scatter_sum(parts):
    keep_a, keep_b, send_a, send_b = parts
    came_a, came_b = hop(send_a, dc=1), hop(send_b, dc=1)
    sum_a, sum_b = wide(keep_a) + wide(came_a), wide(keep_b) + wide(came_b)
    came_a, came_b = hop(narrow(sum_a[4:]), dx=1), hop(narrow(sum_b[4:]), dy=1)
    sum_a, sum_b = sum_a[:4] + wide(came_a), sum_b[:4] + wide(came_b)
    came_a, came_b = hop(narrow(sum_a[2:]), dy=1), hop(narrow(sum_b[2:]), dx=1)
    sum_a, sum_b = sum_a[:2] + wide(came_a), sum_b[:2] + wide(came_b)
    near = hop(narrow(sum_a[1]), dz=1)
    far = hop(narrow(sum_b[0]), dz=2)
    across = hop(narrow(sum_b[1]), dz=3)
    return sum_a[0] + wide(near) + wide(far) + wide(across)


def butterfly(value):
    for flip in ({"dc": 1}, {"dx": 1}, {"dy": 1}, {"dz": 1}, {"dz": 2}):
        value = value + hop(value, **flip)
    return value


KEYS = 192


def pair_scores(live, queries, keys, half, scale):
    lanes = lax.broadcasted_iota(jnp.int32, queries.shape, 1) // HEAD_DIM
    mine = jnp.where(lanes == half, queries, jnp.zeros_like(queries))
    raw = lax.dot_general(
        mine, keys, (((1,), (1,)), ((), ())), preferred_element_type=jnp.float32
    )
    scores = jnp.where(live > 0, raw * scale, -1e30)
    top = jnp.max(scores, axis=-1, keepdims=True)
    powers = jnp.exp(scores - top)
    return mine, powers / jnp.sum(powers, axis=-1, keepdims=True)


def attention(queries, pair, live):
    tokens, width = queries.shape
    keys_all = pair.shape[0]
    scale = 1.0 / math.sqrt(HEAD_DIM)
    blocks = width // 128

    def kernel(live_ref, q_ref, k_ref, v_ref, out_ref):
        q, k, v = q_ref[...], k_ref[...], v_ref[...]
        sums = []
        for half in range(2):
            _, probs = pair_scores(live_ref[...], q, k, half, scale)
            sums.append(
                jnp.dot(probs.astype(jnp.bfloat16), v, preferred_element_type=jnp.float32)
            )
        lanes = lax.broadcasted_iota(jnp.int32, q.shape, 1) // HEAD_DIM
        out_ref[...] = jnp.where(lanes == 0, sums[0], sums[1]).astype(jnp.bfloat16)

    return pl.pallas_call(
        kernel,
        name="attention",
        grid=(blocks,),
        out_shape=jax.ShapeDtypeStruct((tokens, width), jnp.bfloat16),
        in_specs=[
            pl.BlockSpec((1, keys_all), lambda p: (0, 0)),
            pl.BlockSpec((tokens, 128), lambda p: (0, p)),
            pl.BlockSpec((keys_all, 128), lambda p: (0, p)),
            pl.BlockSpec((keys_all, 128), lambda p: (0, p + blocks)),
        ],
        out_specs=pl.BlockSpec((tokens, 128), lambda p: (0, p)),
    )(live, queries, pair, pair)


def attention_back(queries, pair, live, grad_att):
    tokens, width = queries.shape
    keys_all = pair.shape[0]
    scale = 1.0 / math.sqrt(HEAD_DIM)
    blocks = width // 128

    def kernel(live_ref, q_ref, k_ref, v_ref, g_ref, dq_ref, own_k, own_v, far_k, far_v, sum_q, sum_v):
        q, k, v, g = q_ref[...], k_ref[...], v_ref[...], g_ref[...]
        dq = dk = dv = None
        for half in range(2):
            mine, probs = pair_scores(live_ref[...], q, k, half, scale)
            lanes = lax.broadcasted_iota(jnp.int32, q.shape, 1) // HEAD_DIM
            grad = jnp.where(lanes == half, g, jnp.zeros_like(g))
            lanes_k = lax.broadcasted_iota(jnp.int32, k.shape, 1) // HEAD_DIM
            key = jnp.where(lanes_k == half, k, jnp.zeros_like(k))
            grad_probs = lax.dot_general(
                grad, v, (((1,), (1,)), ((), ())), preferred_element_type=jnp.float32
            )
            inner = jnp.sum(probs * grad_probs, axis=-1, keepdims=True)
            grad_scores = (probs * (grad_probs - inner) * scale).astype(jnp.bfloat16)
            dq_part = jnp.dot(grad_scores, key, preferred_element_type=jnp.float32)
            dk_part = lax.dot_general(
                grad_scores, mine, (((0,), (0,)), ((), ())), preferred_element_type=jnp.float32
            )
            dv_part = lax.dot_general(
                probs.astype(jnp.bfloat16),
                grad,
                (((0,), (0,)), ((), ())),
                preferred_element_type=jnp.float32,
            )
            if half == 0:
                dq, dk, dv = dq_part, dk_part, dv_part
            else:
                dq, dk, dv = dq + dq_part, dk + dk_part, dv + dv_part
        dq_ref[...] = dq.astype(jnp.bfloat16)
        sum_q[...] = jnp.sum(dq, axis=0, keepdims=True)
        sum_v[...] = jnp.sum(dv, axis=0, keepdims=True)
        own_k[...] = dk[:KEYS]
        own_v[...] = dv[:KEYS]
        far_k[...] = dk[KEYS:].astype(jnp.bfloat16)
        far_v[...] = dv[KEYS:].astype(jnp.bfloat16)

    def column(rows):
        return pl.BlockSpec((rows, 128), lambda p: (0, p))

    return pl.pallas_call(
        kernel,
        name="attention_back",
        grid=(blocks,),
        out_shape=[
            jax.ShapeDtypeStruct((tokens, width), jnp.bfloat16),
            jax.ShapeDtypeStruct((KEYS, width), jnp.float32),
            jax.ShapeDtypeStruct((KEYS, width), jnp.float32),
            jax.ShapeDtypeStruct((KEYS, width), jnp.bfloat16),
            jax.ShapeDtypeStruct((KEYS, width), jnp.bfloat16),
            jax.ShapeDtypeStruct((1, width), jnp.float32),
            jax.ShapeDtypeStruct((1, width), jnp.float32),
        ],
        in_specs=[
            pl.BlockSpec((1, keys_all), lambda p: (0, 0)),
            column(tokens),
            column(keys_all),
            pl.BlockSpec((keys_all, 128), lambda p: (0, p + blocks)),
            column(tokens),
        ],
        out_specs=[
            column(tokens),
            column(KEYS),
            column(KEYS),
            column(KEYS),
            column(KEYS),
            column(1),
            column(1),
        ],
    )(live, queries, pair, pair, grad_att)


def trade(value):
    core, side = lax.axis_index("clip") % 2, lax.axis_index("frame")
    swaps = []
    for base in range(0, 32, 4):
        swaps += [(base + 1, base + 2), (base + 2, base + 1)]
    return jnp.where(core == side, value, lax.ppermute(value, AXES, swaps))


def block_body(
    layer_input,
    w_qkv,
    b_q,
    b_v,
    w_out,
    b_out,
    ln1_gain,
    ln1_bias,
    ln2_gain,
    ln2_bias,
    w_up,
    b_up,
    w_down,
    b_down,
    grad_y,
    pad_mask,
    clip_row,
):
    _, frames, width = layer_input.shape
    me = my_shard()
    core, side = lax.axis_index("clip") % 2, lax.axis_index("frame")
    inputs = trade(layer_input.reshape(frames, width))
    upstream = trade(grad_y.reshape(frames, width))
    row = lax.axis_index("clip") - core + side
    mask = lax.dynamic_slice_in_dim(pad_mask, clip_row[row], 1)
    spare = KEYS - frames
    live_own = jnp.pad(lax.dynamic_slice_in_dim(mask, core * frames, frames, 1), ((0, 0), (0, spare)))
    live_far = jnp.pad(lax.dynamic_slice_in_dim(mask, (1 - core) * frames, frames, 1), ((0, 0), (0, spare)))
    live = jnp.concatenate([live_own, live_far], axis=1)

    piece = b_q.shape[0]
    lines = jnp.stack([b_q, b_v, b_out, ln1_gain, ln1_bias, ln2_gain, ln2_bias, b_down])
    place = (
        lax.broadcasted_iota(jnp.int32, (piece, width), 1)
        == lax.broadcasted_iota(jnp.int32, (piece, width), 0) + me * piece
    ).astype(jnp.bfloat16)
    lines = jnp.dot(lines, place, preferred_element_type=jnp.float32)
    wide_piece = b_up.shape[0]
    ups = lax.dynamic_update_slice(jnp.zeros((32 * wide_piece,), jnp.float32), wide(b_up), (me * wide_piece,))
    rows_up = ups.shape[0] // width
    vectors = butterfly(narrow(jnp.concatenate([lines, ups.reshape(rows_up, width)], axis=0)))
    vectors = wide(vectors)
    query_bias, value_bias, out_bias, gain_one, shift_one, gain_two, shift_two, down_bias = (
        vectors[k : k + 1] for k in range(8)
    )
    up_bias = vectors[8:].reshape(1, rows_up * width)

    qkv_mat = assemble(w_qkv, "whole_qkv")
    out_mat = assemble(w_out, "whole_out")
    up_mat = assemble(w_up, "whole_up")
    down_mat = assemble(w_down, "whole_down")

    inputs_f = wide(inputs)
    normed1, factor1 = normalize(inputs_f)
    hidden1 = narrow(normed1 * gain_one + shift_one)
    projected = matmul(hidden1, qkv_mat)
    queries = narrow(projected[:, :width] + query_bias)
    keys_local = projected[:, width : 2 * width]
    values_local = projected[:, 2 * width :] + value_bias
    pair_local = jnp.pad(
        narrow(jnp.concatenate([keys_local, values_local], axis=-1)), ((0, spare), (0, 0))
    )
    pair = jnp.concatenate([pair_local, hop(pair_local, dc=1)], axis=0)
    attended_b = attention(queries, pair, live)
    resid = inputs_f + matmul(attended_b, out_mat) + out_bias
    normed2, factor2 = normalize(resid)
    hidden2 = narrow(normed2 * gain_two + shift_two)
    pre = matmul(hidden2, up_mat) + up_bias
    act = narrow(gelu_exact(pre))
    grad_down = scatter_sum(weight_grad(act, upstream, 256, "grad_down"))
    output = trade(narrow(resid + matmul(act, down_mat) + down_bias))

    upstream_f = wide(upstream)
    grad_down_bias = jnp.sum(upstream_f, axis=0, keepdims=True)
    grad_pre = lax.dot_general(
        upstream, down_mat, (((1,), (1,)), ((), ())), preferred_element_type=jnp.float32
    ) * gelu_slope(pre)
    grad_pre_b = narrow(grad_pre)
    grad_up_bias = jnp.sum(grad_pre, axis=0).reshape(rows_up, width)
    grad_up = scatter_sum(weight_grad(hidden2, grad_pre_b, 768, "grad_up"))
    grad_hidden2 = lax.dot_general(
        grad_pre_b, up_mat, (((1,), (1,)), ((), ())), preferred_element_type=jnp.float32
    )
    grad_gain_two = jnp.sum(grad_hidden2 * normed2, axis=0, keepdims=True)
    grad_shift_two = jnp.sum(grad_hidden2, axis=0, keepdims=True)
    grad_resid = upstream_f + norm_back(grad_hidden2 * gain_two, normed2, factor2)
    grad_resid_b = narrow(grad_resid)
    grad_out_bias = jnp.sum(grad_resid, axis=0, keepdims=True)
    grad_out = scatter_sum(weight_grad(attended_b, grad_resid_b, 768, "grad_out"))
    grad_att = narrow(
        lax.dot_general(
            grad_resid_b, out_mat, (((1,), (1,)), ((), ())), preferred_element_type=jnp.float32
        )
    )
    grad_queries, own_k, own_v, far_k, far_v, grad_query_bias, grad_value_bias = attention_back(
        queries, pair, live, grad_att
    )
    grad_keys = narrow(own_k + wide(hop(far_k, dc=1)))[:frames]
    grad_values = narrow(own_v + wide(hop(far_v, dc=1)))[:frames]
    grad_proj = jnp.concatenate([grad_queries, grad_keys, grad_values], axis=-1)
    grad_qkv = scatter_sum(weight_grad(hidden1, grad_proj, 768, "grad_qkv"))
    grad_hidden1 = lax.dot_general(
        grad_proj, qkv_mat, (((1,), (1,)), ((), ())), preferred_element_type=jnp.float32
    )
    grad_gain_one = jnp.sum(grad_hidden1 * normed1, axis=0, keepdims=True)
    grad_shift_one = jnp.sum(grad_hidden1, axis=0, keepdims=True)
    grad_input = grad_resid + norm_back(grad_hidden1 * gain_one, normed1, factor1)
    grad_input = jnp.where(core == side, grad_input, wide(trade(narrow(grad_input))))

    early = butterfly(
        jnp.concatenate(
            [grad_out_bias, grad_gain_two, grad_shift_two, grad_down_bias, grad_up_bias], axis=0
        )
    )
    late = butterfly(
        jnp.concatenate([grad_query_bias, grad_value_bias, grad_gain_one, grad_shift_one], axis=0)
    )
    mine_early = lax.dynamic_slice_in_dim(early[:4], me * piece, piece, 1)
    mine_late = lax.dynamic_slice_in_dim(late, me * piece, piece, 1)
    mine_up = lax.dynamic_slice_in_dim(early[4:].reshape(-1), me * wide_piece, wide_piece)
    return (
        output[None],
        grad_input[None],
        grad_qkv,
        mine_late[0],
        mine_late[1],
        grad_out,
        mine_early[0],
        mine_late[2],
        mine_late[3],
        mine_early[1],
        mine_early[2],
        grad_up,
        mine_up,
        grad_down,
        mine_early[3],
    )


def solution(mesh):
    grid = (mesh.shape["clip"], mesh.shape["frame"])
    body = block_body if grid == (16, 2) else general_body
    return jax.shard_map(
        body,
        mesh=mesh,
        in_specs=(
            P("clip", "frame", None),
            P(("clip", "frame"), None),
            P(("clip", "frame")),
            P(("clip", "frame")),
            P(("clip", "frame"), None),
            P(("clip", "frame")),
            P(("clip", "frame")),
            P(("clip", "frame")),
            P(("clip", "frame")),
            P(("clip", "frame")),
            P(("clip", "frame"), None),
            P(("clip", "frame")),
            P(("clip", "frame"), None),
            P(("clip", "frame")),
            P("clip", "frame", None),
            P(),
            P(),
        ),
        out_specs=(
            P("clip", "frame", None),
            P("clip", "frame", None),
            P(("clip", "frame"), None),
            P(("clip", "frame")),
            P(("clip", "frame")),
            P(("clip", "frame"), None),
            P(("clip", "frame")),
            P(("clip", "frame")),
            P(("clip", "frame")),
            P(("clip", "frame")),
            P(("clip", "frame")),
            P(("clip", "frame"), None),
            P(("clip", "frame")),
            P(("clip", "frame"), None),
            P(("clip", "frame")),
        ),
        check_vma=False,
    )
```
